128 devices in a mesh: blk: 16 (over y_hi, x, core), occ: 8 (over z, y_lo).
Axes of the slice: x: 4, y: 4 (y_hi: 2, y_lo: 2; y = y_hi * 2 + y_lo), z: 4, core: 2. Of those that a mesh axis runs over, the one named last changes fastest.
Arguments:
- amplitudes: bfloat16 [8, 512, 163840], P(None, 'blk', 'occ'), may hold values from -6 to 6
- cholesky: bfloat16 [4096, 4096], P('occ'), may hold values from -0.09375 to 0.09375
- virtual_order: int32 [64], replicated, may hold values from 0 to 63, each once
Outputs:
- residual: bfloat16 [8, 512, 163840], P(None, 'blk', 'occ')
The draws below stay inside these ranges and needn't reach their ends.
Inputs may be any that keep to these rules, and one draw needn't show every extreme that they name: The orbitals of irrep h are virtual_order[h * 8 + u] for u < 8; every orbital appears once.
All inputs are finite; a program needn't handle non-finite values.
Results may differ from the reference program's by a relative error of at most 0.0051.
Values may be sent and summed in bfloat16 or wider, within the bound.
A program may use at most 192 MiB of HBM per device.

```python
import jax
import jax.numpy as jnp
import numpy as np

NQ = 4096
NV = 64
SLOTS = 512
NPG = 163840


def level_of(stream_key, dims, split, smallest, top_value):
    def one(axis_at, parts):
        heights = jax.random.uniform(jax.random.fold_in(jax.random.fold_in(stream_key, 6), axis_at), (parts,), jnp.float32, smallest / len(split), top_value / len(split))
        return jnp.repeat(jnp.exp(heights), dims[axis_at] // parts).reshape((-1,) + (1,) * (len(dims) - axis_at - 1))

    factor_of = one(*split[0])
    for cut in split[1:]:
        factor_of = factor_of * one(*cut)
    return factor_of


def centred(key, dims, deviation, most, shards=(), kind=jnp.bfloat16):
    level = level_of(key, dims, shards, -0.22, 0.18) if shards else 1.0
    values = jax.random.normal(key, dims, jnp.float32) * deviation * level
    return jnp.minimum(jnp.maximum(values, -most), most).astype(kind)


def setup_inputs(seed: int = 0) -> dict:
    arg_keys = jax.random.split(jax.random.key(seed), 4)
    return {
        "amplitudes": centred(arg_keys[0], (8, SLOTS, NPG), 1.0, 6.0, ((1, 16), (2, 8))),
        "cholesky": centred(arg_keys[1], (NQ, NV * NV), NQ ** -0.5, 0.09375, ((0, 8),)),
        "virtual_order": jax.random.permutation(arg_keys[2], NV).astype(jnp.int32),
    }


def reference(amplitudes, cholesky, virtual_order):
    vir_count = virtual_order.shape[0]
    per_irrep = vir_count // 8
    slot_count = vir_count * per_irrep
    vectors = cholesky.reshape(cholesky.shape[0], vir_count, vir_count)
    sorted_vec = jnp.take(jnp.take(vectors, virtual_order, axis=1), virtual_order, axis=2)
    blocks = sorted_vec.astype(jnp.float32).reshape(cholesky.shape[0], 8, per_irrep, 8, per_irrep)
    outputs = []
    for symmetry in range(8):
        partner = np.arange(8) ^ symmetry
        paired = blocks[:, partner][:, :, :, partner]
        integrals = jnp.einsum("qhukx,qhwky->huwkxy", blocks, paired)
        integrals = integrals.reshape(slot_count, slot_count).astype(jnp.bfloat16)
        ladder = jnp.dot(integrals, amplitudes[symmetry], preferred_element_type=jnp.float32)
        outputs.append(ladder.astype(jnp.bfloat16))
    return jnp.stack(outputs)
```

```python
import functools

import jax
import jax.numpy as jnp
from jax import lax
from jax.experimental import pallas as pl
from jax.experimental.pallas import tpu as pltpu
from jax.sharding import PartitionSpec as P

MESH = pl.DeviceIdType.MESH
CHUNKS = 8
FIRST, SECOND = 4, 6
HOPS = ((0, 1), (0, 3), (1, 0), (0, 2), (1, 1), (1, 3), (1, 2), (0, 0))
PEERS = tuple((dy, dx, dc) for dc in (0, 1) for dy, dx in HOPS if (dy, dx, dc) != (0, 0, 0))
NT = (((1,), (1,)), ((), ()))


def xor8(a, b):
    return sum(2**i * ((a // 2**i % 2 + b // 2**i % 2) % 2) for i in range(3))


def dot(a, b, dims=(((1,), (0,)), ((), ()))):
    return lax.dot_general(a, b, dims, preferred_element_type=jnp.float32)


def iota(shape, axis):
    return lax.broadcasted_iota(jnp.int32, shape, axis)


def kernel(
    order, amp, chol, res,
    slots, out, vec, srt, brow, arow, gram, part, gath, mine, full, ints,
    in_s, in_r, back_s, back_r, red_s, red_r, all_s, all_r, own_in, own_out, vec_sem,
):
    blk, occ = lax.axis_index("blk"), lax.axis_index("occ")
    y_hi, x_at, core = blk // 8, blk // 2 % 4, blk % 2
    sym = blk // 2
    width = slots.shape[1]
    step = width // CHUNKS
    rows = slots.shape[0] // 16

    def peer(offset):
        dy, dx, dc = offset
        return (y_hi + dy) % 2 * 8 + (x_at + dx) % 4 * 2 + (core + dc) % 2

    def occ_peer(d, e):
        return {"blk": sym * 2 + (core + e) % 2, "occ": (occ + d) % 8}

    others = [(d, e) for e in (0, 1) for d in range(8) if (d, e) != (0, 0)]

    load = pltpu.make_async_copy(chol, vec, vec_sem)
    load.start()
    keep = pltpu.make_async_copy(
        amp.at[sym, :, pl.ds(pl.multiple_of(core * width, 128), width)],
        slots.at[pl.ds(pl.multiple_of(blk * rows, 32), rows), :],
        own_in,
    )
    keep.start()

    barrier = pltpu.get_barrier_semaphore()
    for offset in PEERS:
        pl.semaphore_signal(barrier, inc=1, device_id={"blk": peer(offset)}, device_id_type=MESH)
    for d, e in others:
        if d:
            pl.semaphore_signal(barrier, inc=1, device_id=occ_peer(d, e), device_id_type=MESH)
    pl.semaphore_wait(barrier, len(PEERS) + 14)

    def columns(half, s):
        return pl.ds(pl.multiple_of(half * width + s * step, 128), step)

    def block(at):
        return pl.ds(pl.multiple_of(at * rows, 32), rows)

    def send_in(i, s):
        to = peer(PEERS[i])
        return pltpu.make_async_remote_copy(
            src_ref=amp.at[to // 2, :, columns(to % 2, s)],
            dst_ref=slots.at[block(blk), columns(0, s)],
            send_sem=in_s.at[i, s],
            recv_sem=in_r.at[i, s],
            device_id={"blk": to},
            device_id_type=MESH,
        )

    def send_back(i, s):
        to = peer(PEERS[i])
        return pltpu.make_async_remote_copy(
            src_ref=out.at[block(to), columns(0, s)],
            dst_ref=res.at[sym, :, columns(core, s)],
            send_sem=back_s.at[i, s],
            recv_sem=back_r.at[i, s],
            device_id={"blk": to},
            device_id_type=MESH,
        )

    def keep_back(s):
        return pltpu.make_async_copy(
            out.at[block(blk), columns(0, s)], res.at[sym, :, columns(core, s)], own_out.at[s]
        )

    def start_in(first, last):
        @pl.loop(first, last)
        def _(s):
            for i in range(len(PEERS)):
                send_in(i, s).start()

    start_in(0, FIRST)

    target = iota((256, 1), 0)
    picked = jnp.zeros((256, 1), jnp.int32)
    for m in range(64):
        picked = jnp.where(target % 64 == m, order[m], picked)
    choose = iota((256, 256), 1) == picked + target // 64 * 64
    choose = choose.astype(jnp.float32).astype(jnp.bfloat16)
    load.wait()

    @pl.loop(0, 16)
    def _(j):
        at = pl.ds(pl.multiple_of(j * 256, 256), 256)
        sorted_vec = dot(choose, vec[:, at], NT).astype(jnp.bfloat16)
        for a in range(4):
            srt[j * 4 + a] = sorted_vec[a * 64 : a * 64 + 64]

    def orbital(irrep, u):
        return srt[order[irrep * 8 + u]]

    lane = iota((8, 1024), 1)
    for local in range(2):
        pair = core * 2 + local

        @pl.loop(0, 8)
        def _(w):
            for h in range(2):
                at = pl.ds(pl.multiple_of(w * 128 + h * 64, 64), 64)
                brow[at, :] = orbital(xor8(pair * 2 + h, sym), w)

        @pl.loop(0, 8)
        def _(u):
            for h in range(2):
                arow[h * 64 : h * 64 + 64, :] = orbital(pair * 2 + h, u)
            product = dot(arow[...], brow[...], NT)
            wanted = lane // 8 % 16
            total = jnp.zeros((8, 1024), jnp.float32)
            for h in range(2):
                for k in range(8):
                    at = h * 64 + k * 8
                    total = jnp.where(wanted == h * 8 + xor8(k, sym), product[at : at + 8], total)
            for w in range(8):
                gram[w, pl.ds(pl.multiple_of(u * 8, 8), 8), :] = total[:, w * 128 : w * 128 + 128]

        for x in range(8):
            for w in range(8):
                part[local * 64 + w * 8 : local * 64 + w * 8 + 8, x * 128 : x * 128 + 128] = gram[
                    w, pl.ds(x, 8, stride=8), :
                ]

    def slice_of(at):
        return pl.ds(pl.multiple_of(at * 16, 16), 16)

    def reduce_to(d):
        return pltpu.make_async_remote_copy(
            src_ref=part.at[slice_of((occ + d) % 8), :],
            dst_ref=gath.at[d - 1],
            send_sem=red_s.at[d],
            recv_sem=red_r.at[d],
            device_id=occ_peer(d, 0),
            device_id_type=MESH,
        )

    for d in range(1, 8):
        reduce_to(d).start()
    start_in(FIRST, SECOND)
    total = part[slice_of(occ), :]
    for d in range(1, 8):
        reduce_to(d).wait_recv()
        total = total + gath[d - 1]
    mine[...] = total.astype(jnp.bfloat16)
    place = pl.ds(pl.multiple_of(core * 128 + occ * 16, 16), 16)
    full[place, :] = total.astype(jnp.bfloat16)

    def share(n):
        d, e = others[n]
        return pltpu.make_async_remote_copy(
            src_ref=mine,
            dst_ref=full.at[place, :],
            send_sem=all_s.at[n],
            recv_sem=all_r.at[n],
            device_id=occ_peer(d, e),
            device_id_type=MESH,
        )

    for n in range(len(others)):
        share(n).start()
    start_in(SECOND, CHUNKS)
    for n in range(len(others)):
        share(n).wait_recv()

    goal, source = iota((1024, 512), 1), iota((1024, 512), 0)
    gk = goal // 64
    other = sum(2**i * ((gk // 2**i % 2 + sym // 2**i % 2) % 2) for i in range(3))
    base = goal // 8 % 8 * 128 + other * 8 + goal % 8
    r, c = iota((256, 256), 0), iota((256, 256), 1)
    swap = c == r // 64 * 64 + r % 8 * 8 + r // 8 % 8
    swap = swap.astype(jnp.float32).astype(jnp.bfloat16)
    for h in range(2):
        pick = (source == base + h * 64).astype(jnp.float32).astype(jnp.bfloat16)
        moved = dot(full[...], pick).astype(jnp.bfloat16)
        moved = dot(swap, moved).astype(jnp.bfloat16)
        for pair in range(4):
            at = (pair * 2 + h) * 64
            ints[at : at + 64, :] = moved[pair * 64 : pair * 64 + 64]

    keep.wait()

    @pl.loop(0, CHUNKS)
    def _(s):
        for i in range(len(PEERS)):
            send_in(i, s).wait_recv()

        @pl.loop(0, step // 256)
        def _(j):
            at = pl.ds(pl.multiple_of(s * step + j * 256, 256), 256)
            out[:, at] = dot(ints[...], slots[:, at]).astype(jnp.bfloat16)

        for i in range(len(PEERS)):
            send_back(i, s).start()
        keep_back(s).start()

    for d in range(1, 8):
        reduce_to(d).wait_send()
    for n in range(len(others)):
        share(n).wait_send()

    @pl.loop(0, CHUNKS)
    def _(s):
        for i in range(len(PEERS)):
            send_in(i, s).wait_send()
        for i in range(len(PEERS)):
            send_back(i, s).wait()
        keep_back(s).wait()


def body(amplitudes, cholesky, virtual_order):
    groups, rows, columns = amplitudes.shape
    width = columns // 2
    sems = pltpu.SemaphoreType.DMA
    peers = len(PEERS)
    vectors = cholesky.shape[0]
    return pl.pallas_call(
        kernel,
        out_shape=jax.ShapeDtypeStruct(amplitudes.shape, jnp.bfloat16),
        in_specs=[
            pl.BlockSpec(memory_space=pltpu.SMEM),
            pl.BlockSpec(memory_space=pl.ANY),
            pl.BlockSpec(memory_space=pl.ANY),
        ],
        out_specs=pl.BlockSpec(memory_space=pl.ANY),
        scratch_shapes=[
            pltpu.VMEM((16 * rows, width), jnp.bfloat16),
            pltpu.VMEM((16 * rows, width), jnp.bfloat16),
            pltpu.VMEM(cholesky.shape, jnp.bfloat16),
            pltpu.VMEM((64, 64, vectors), jnp.bfloat16),
            pltpu.VMEM((1024, vectors), jnp.bfloat16),
            pltpu.VMEM((128, vectors), jnp.bfloat16),
            pltpu.VMEM((8, 64, 128), jnp.float32),
            pltpu.VMEM((128, 1024), jnp.float32),
            pltpu.VMEM((7, 16, 1024), jnp.float32),
            pltpu.VMEM((16, 1024), jnp.bfloat16),
            pltpu.VMEM((256, 1024), jnp.bfloat16),
            pltpu.VMEM((512, 512), jnp.bfloat16),
            sems((peers, CHUNKS)),
            sems((peers, CHUNKS)),
            sems((peers, CHUNKS)),
            sems((peers, CHUNKS)),
            sems((8,)),
            sems((8,)),
            sems((15,)),
            sems((15,)),
            sems,
            sems((CHUNKS,)),
            sems,
        ],
        compiler_params=pltpu.CompilerParams(
            collective_id=0, has_side_effects=True, vmem_limit_bytes=64000 * 1024
        ),
        name="ladder",
    )(virtual_order, amplitudes, cholesky)


def solution(mesh):
    placed = (P(None, "blk", "occ"), P("occ", None), P())
    return jax.shard_map(
        body, mesh=mesh, in_specs=placed, out_specs=P(None, "blk", "occ"), check_vma=False
    )
```

```python
import functools

import jax
import jax.numpy as jnp
from jax import lax
from jax.experimental import pallas as pl
from jax.experimental.pallas import tpu as pltpu
from jax.sharding import PartitionSpec as P

MESH = pl.DeviceIdType.MESH
CHUNKS = 8
FIRST, SECOND = 4, 6
HOPS = ((0, 1), (0, 3), (1, 0), (0, 2), (1, 1), (1, 3), (1, 2), (0, 0))
PEERS = tuple((dy, dx, dc) for dc in (0, 1) for dy, dx in HOPS if (dy, dx, dc) != (0, 0, 0))
NT = (((1,), (1,)), ((), ()))


def xor8(a, b):
    return sum(2**i * ((a // 2**i % 2 + b // 2**i % 2) % 2) for i in range(3))


def dot(a, b, dims=(((1,), (0,)), ((), ()))):
    return lax.dot_general(a, b, dims, preferred_element_type=jnp.float32)


def iota(shape, axis):
    return lax.broadcasted_iota(jnp.int32, shape, axis)


def kernel(
    orbitals, amp, chol, res,
    order, slots, out, vec, srt, brow, arow, gram, part, gath, mine, full, ints,
    in_s, in_r, back_s, back_r, red_s, red_r, all_s, all_r, own_in, own_out, vec_sem, order_sem,
):
    blk, occ = lax.axis_index("blk"), lax.axis_index("occ")
    y_hi, x_at, core = blk // 8, blk // 2 % 4, blk % 2
    sym, z_at = blk // 2, occ // 2
    width = slots.shape[1]
    step = width // CHUNKS
    rows = slots.shape[0] // 16

    def peer(offset):
        dy, dx, dc = offset
        return (y_hi + dy) % 2 * 8 + (x_at + dx) % 4 * 2 + (core + dc) % 2

    def near(d, f, e):
        return {"blk": sym * 2 + (core + e) % 2, "occ": (z_at + d) % 4 * 2 + (occ + f) % 2}

    others = [(d, e) for e in (0, 1) for d in range(4) if (d, e) != (0, 0)]

    load = pltpu.make_async_copy(chol, vec, vec_sem)
    load.start()
    read = pltpu.make_async_copy(orbitals, order, order_sem)
    read.start()
    keep = pltpu.make_async_copy(
        amp.at[sym, :, pl.ds(pl.multiple_of(core * width, 128), width)],
        slots.at[pl.ds(pl.multiple_of(blk * rows, 32), rows), :],
        own_in,
    )
    keep.start()

    barrier = pltpu.get_barrier_semaphore()
    for offset in PEERS:
        pl.semaphore_signal(barrier, inc=1, device_id={"blk": peer(offset)}, device_id_type=MESH)
    around = [(d, 0, e) for d, e in others if d] + [(0, 1, 0)]
    for at in around:
        pl.semaphore_signal(barrier, inc=1, device_id=near(*at), device_id_type=MESH)
    pl.semaphore_wait(barrier, len(PEERS) + len(around))

    def columns(half, s):
        return pl.ds(pl.multiple_of(half * width + s * step, 128), step)

    def block(at):
        return pl.ds(pl.multiple_of(at * rows, 32), rows)

    def send_in(i, s):
        to = peer(PEERS[i])
        return pltpu.make_async_remote_copy(
            src_ref=amp.at[to // 2, :, columns(to % 2, s)],
            dst_ref=slots.at[block(blk), columns(0, s)],
            send_sem=in_s.at[i, s],
            recv_sem=in_r.at[i, s],
            device_id={"blk": to},
            device_id_type=MESH,
        )

    def send_back(i, s):
        to = peer(PEERS[i])
        return pltpu.make_async_remote_copy(
            src_ref=out.at[block(to), columns(0, s)],
            dst_ref=res.at[sym, :, columns(core, s)],
            send_sem=back_s.at[i, s],
            recv_sem=back_r.at[i, s],
            device_id={"blk": to},
            device_id_type=MESH,
        )

    def keep_back(s):
        return pltpu.make_async_copy(
            out.at[block(blk), columns(0, s)], res.at[sym, :, columns(core, s)], own_out.at[s]
        )

    def start_in(first, last):
        @pl.loop(first, last)
        def _(s):
            for i in range(len(PEERS)):
                send_in(i, s).start()

    start_in(0, FIRST)

    read.wait()
    target = iota((256, 1), 0)
    picked = jnp.zeros((256, 1), jnp.int32)
    for m in range(64):
        picked = jnp.where(target % 64 == m, order[m], picked)
    choose = iota((256, 256), 1) == picked + target // 64 * 64
    choose = choose.astype(jnp.float32).astype(jnp.bfloat16)
    load.wait()

    @pl.loop(0, 16)
    def _(j):
        at = pl.ds(pl.multiple_of(j * 256, 256), 256)
        sorted_vec = dot(choose, vec[:, at], NT).astype(jnp.bfloat16)
        for a in range(4):
            srt[j * 4 + a] = sorted_vec[a * 64 : a * 64 + 64]

    def orbital(irrep, u):
        return srt[order[irrep * 8 + u]]

    lane = iota((8, 1024), 1)
    for local in range(2):
        pair = core * 2 + local

        @pl.loop(0, 8)
        def _(w):
            for h in range(2):
                at = pl.ds(pl.multiple_of(w * 128 + h * 64, 64), 64)
                brow[at, :] = orbital(xor8(pair * 2 + h, sym), w)

        @pl.loop(0, 8)
        def _(u):
            for h in range(2):
                arow[h * 64 : h * 64 + 64, :] = orbital(pair * 2 + h, u)
            product = dot(arow[...], brow[...], NT)
            wanted = lane // 8 % 16
            total = jnp.zeros((8, 1024), jnp.float32)
            for h in range(2):
                for k in range(8):
                    at = h * 64 + k * 8
                    total = jnp.where(wanted == h * 8 + xor8(k, sym), product[at : at + 8], total)
            for w in range(8):
                gram[w, pl.ds(pl.multiple_of(u * 8, 8), 8), :] = total[:, w * 128 : w * 128 + 128]

        for x in range(8):
            for w in range(8):
                part[local * 64 + w * 8 : local * 64 + w * 8 + 8, x * 128 : x * 128 + 128] = gram[
                    w, pl.ds(x, 8, stride=8), :
                ]

    def rows_of(at):
        return pl.ds(pl.multiple_of(at * 32, 32), 32)

    def along_z(d):
        return pltpu.make_async_remote_copy(
            src_ref=part.at[rows_of((z_at + d) % 4), :],
            dst_ref=gath.at[d - 1],
            send_sem=red_s.at[d],
            recv_sem=red_r.at[d],
            device_id=near(d, 0, 0),
            device_id_type=MESH,
        )

    for d in range(1, 4):
        along_z(d).start()
    total = part[rows_of(z_at), :]
    for d in range(1, 4):
        along_z(d).wait_recv()
        total = total + gath[d - 1]
    mine[...] = total
    along_y = pltpu.make_async_remote_copy(
        src_ref=mine,
        dst_ref=gath.at[3],
        send_sem=red_s.at[0],
        recv_sem=red_r.at[0],
        device_id=near(0, 1, 0),
        device_id_type=MESH,
    )
    along_y.start()
    start_in(FIRST, SECOND)
    along_y.wait_recv()
    place = pl.ds(pl.multiple_of(core * 128 + z_at * 32, 32), 32)
    full[place, :] = (mine[...] + gath[3]).astype(jnp.bfloat16)

    def share(n):
        d, e = others[n]
        return pltpu.make_async_remote_copy(
            src_ref=full.at[place, :],
            dst_ref=full.at[place, :],
            send_sem=all_s.at[n],
            recv_sem=all_r.at[n],
            device_id=near(d, 0, e),
            device_id_type=MESH,
        )

    for n in range(len(others)):
        share(n).start()
    start_in(SECOND, CHUNKS)
    for n in range(len(others)):
        share(n).wait_recv()

    goal, source = iota((1024, 512), 1), iota((1024, 512), 0)
    gk = goal // 64
    other = sum(2**i * ((gk // 2**i % 2 + sym // 2**i % 2) % 2) for i in range(3))
    base = goal // 8 % 8 * 128 + other * 8 + goal % 8
    r, c = iota((256, 256), 0), iota((256, 256), 1)
    swap = c == r // 64 * 64 + r % 8 * 8 + r // 8 % 8
    swap = swap.astype(jnp.float32).astype(jnp.bfloat16)
    for h in range(2):
        pick = (source == base + h * 64).astype(jnp.float32).astype(jnp.bfloat16)
        moved = dot(full[...], pick).astype(jnp.bfloat16)
        moved = dot(swap, moved).astype(jnp.bfloat16)
        for pair in range(4):
            at = (pair * 2 + h) * 64
            ints[at : at + 64, :] = moved[pair * 64 : pair * 64 + 64]

    keep.wait()

    @pl.loop(0, CHUNKS)
    def _(s):
        for i in range(len(PEERS)):
            send_in(i, s).wait_recv()

        @pl.loop(0, step // 256)
        def _(j):
            at = pl.ds(pl.multiple_of(s * step + j * 256, 256), 256)
            out[:, at] = dot(ints[...], slots[:, at]).astype(jnp.bfloat16)

        for i in range(len(PEERS)):
            send_back(i, s).start()
        keep_back(s).start()

    for d in range(1, 4):
        along_z(d).wait_send()
    along_y.wait_send()
    for n in range(len(others)):
        share(n).wait_send()

    @pl.loop(0, CHUNKS)
    def _(s):
        for i in range(len(PEERS)):
            send_in(i, s).wait_send()
        for i in range(len(PEERS)):
            send_back(i, s).wait()
        keep_back(s).wait()


def body(amplitudes, cholesky, virtual_order):
    groups, rows, columns = amplitudes.shape
    width = columns // 2
    sems = pltpu.SemaphoreType.DMA
    peers = len(PEERS)
    vectors = cholesky.shape[0]
    return pl.pallas_call(
        kernel,
        out_shape=pltpu.VMEM(amplitudes.shape, jnp.bfloat16),
        in_specs=[
            pl.BlockSpec(memory_space=pl.ANY),
            pl.BlockSpec(memory_space=pl.ANY),
            pl.BlockSpec(memory_space=pl.ANY),
        ],
        out_specs=pl.BlockSpec(memory_space=pl.ANY),
        scratch_shapes=[
            pltpu.SMEM(virtual_order.shape, jnp.int32),
            pltpu.VMEM((16 * rows, width), jnp.bfloat16),
            pltpu.VMEM((16 * rows, width), jnp.bfloat16),
            pltpu.VMEM(cholesky.shape, jnp.bfloat16),
            pltpu.VMEM((64, 64, vectors), jnp.bfloat16),
            pltpu.VMEM((1024, vectors), jnp.bfloat16),
            pltpu.VMEM((128, vectors), jnp.bfloat16),
            pltpu.VMEM((8, 64, 128), jnp.float32),
            pltpu.VMEM((128, 1024), jnp.float32),
            pltpu.VMEM((4, 32, 1024), jnp.float32),
            pltpu.VMEM((32, 1024), jnp.float32),
            pltpu.VMEM((256, 1024), jnp.bfloat16),
            pltpu.VMEM((512, 512), jnp.bfloat16),
            sems((peers, CHUNKS)),
            sems((peers, CHUNKS)),
            sems((peers, CHUNKS)),
            sems((peers, CHUNKS)),
            sems((4,)),
            sems((4,)),
            sems((7,)),
            sems((7,)),
            sems,
            sems((CHUNKS,)),
            sems,
            sems,
        ],
        compiler_params=pltpu.CompilerParams(
            collective_id=0, has_side_effects=True, vmem_limit_bytes=44000 * 1024
        ),
        name="ladder",
    )(pltpu.with_memory_space_constraint(virtual_order, pltpu.HBM), amplitudes, pltpu.with_memory_space_constraint(cholesky, pltpu.HBM))


def solution(mesh):
    placed = (P(None, "blk", "occ"), P("occ", None), P())
    return jax.shard_map(
        body, mesh=mesh, in_specs=placed, out_specs=P(None, "blk", "occ"), check_vma=False
    )
```

```python
import functools

import jax
import jax.numpy as jnp
from jax import lax
from jax.experimental import pallas as pl
from jax.experimental.pallas import tpu as pltpu
from jax.sharding import PartitionSpec as P

MESH = pl.DeviceIdType.MESH
CHUNKS = 8
EARLY, FIRST, SECOND = 2, 4, 6
HOPS = ((0, 1), (0, 3), (1, 0), (0, 2), (1, 1), (1, 3), (1, 2), (0, 0))
PEERS = tuple((dy, dx, dc) for dc in (0, 1) for dy, dx in HOPS if (dy, dx, dc) != (0, 0, 0))
NEAR = [i for i, at in enumerate(PEERS) if at[:2] in ((0, 1), (0, 3), (1, 0), (0, 0))]
MIDDLE = [i for i, at in enumerate(PEERS) if at[:2] in ((0, 2), (1, 1), (1, 3))]
FAR = [i for i, at in enumerate(PEERS) if at[:2] == (1, 2)]
NT = (((1,), (1,)), ((), ()))


def xor8(a, b):
    return sum(2**i * ((a // 2**i % 2 + b // 2**i % 2) % 2) for i in range(3))


def dot(a, b, dims=(((1,), (0,)), ((), ()))):
    return lax.dot_general(a, b, dims, preferred_element_type=jnp.float32)


def iota(shape, axis):
    return lax.broadcasted_iota(jnp.int32, shape, axis)


def kernel(
    orbitals, amp, chol, res,
    order, slots, out, vec, srt, brow, arow, gram, part, gath, mine, full, ints,
    in_s, in_r, back_s, back_r, red_s, red_r, all_s, all_r, own_in, own_out, vec_sem, order_sem,
    x_sem, z_sem, far_sem,
):
    blk, occ = lax.axis_index("blk"), lax.axis_index("occ")
    y_hi, x_at, core = blk // 8, blk // 2 % 4, blk % 2
    sym, z_at = blk // 2, occ // 2
    width = slots.shape[1]
    step = width // CHUNKS
    rows = slots.shape[0] // 16

    def peer(offset):
        dy, dx, dc = offset
        return (y_hi + dy) % 2 * 8 + (x_at + dx) % 4 * 2 + (core + dc) % 2

    def near(d, f, e):
        return {"blk": sym * 2 + (core + e) % 2, "occ": (z_at + d) % 4 * 2 + (occ + f) % 2}

    others = [(d, e) for e in (0, 1) for d in range(4) if (d, e) != (0, 0)]

    load = pltpu.make_async_copy(chol, vec, vec_sem)
    load.start()
    read = pltpu.make_async_copy(orbitals, order, order_sem)
    read.start()
    keep = pltpu.make_async_copy(
        amp.at[sym, :, pl.ds(pl.multiple_of(core * width, 128), width)],
        slots.at[pl.ds(pl.multiple_of(blk * rows, 32), rows), :],
        own_in,
    )
    keep.start()

    def signal(sem, device):
        pl.semaphore_signal(sem, inc=1, device_id=device, device_id_type=MESH)

    barrier = pltpu.get_barrier_semaphore()
    for i in NEAR:
        signal(barrier, {"blk": peer(PEERS[i])})
    for d, f in ((1, 0), (3, 0), (0, 1)):
        signal(barrier, near(d, f, 0))
    pl.semaphore_wait(barrier, len(NEAR) + 3)

    def columns(half, s):
        return pl.ds(pl.multiple_of(half * width + s * step, 128), step)

    def block(at):
        return pl.ds(pl.multiple_of(at * rows, 32), rows)

    def send_in(i, s):
        to = peer(PEERS[i])
        return pltpu.make_async_remote_copy(
            src_ref=amp.at[to // 2, :, columns(to % 2, s)],
            dst_ref=slots.at[block(blk), columns(0, s)],
            send_sem=in_s.at[i, s],
            recv_sem=in_r.at[i, s],
            device_id={"blk": to},
            device_id_type=MESH,
        )

    def send_back(i, s):
        to = peer(PEERS[i])
        return pltpu.make_async_remote_copy(
            src_ref=out.at[block(to), columns(0, s)],
            dst_ref=res.at[sym, :, columns(core, s)],
            send_sem=back_s.at[i, s],
            recv_sem=back_r.at[i, s],
            device_id={"blk": to},
            device_id_type=MESH,
        )

    def keep_back(s):
        return pltpu.make_async_copy(
            out.at[block(blk), columns(0, s)], res.at[sym, :, columns(core, s)], own_out.at[s]
        )

    def start_in(first, last, which=range(len(PEERS))):
        @pl.loop(first, last)
        def _(s):
            for i in which:
                send_in(i, s).start()

    start_in(0, EARLY, NEAR)
    for dx in (1, 3):
        signal(x_sem, {"blk": peer((0, dx, 0))})
        signal(z_sem, near(dx, 0, 0))
    pl.semaphore_wait(x_sem, 2)
    start_in(0, EARLY, MIDDLE)
    signal(far_sem, {"blk": peer((0, 3, 0))})
    pl.semaphore_wait(far_sem, 1)
    start_in(0, EARLY, FAR)
    start_in(EARLY, FIRST)

    read.wait()
    target = iota((256, 1), 0)
    picked = jnp.zeros((256, 1), jnp.int32)
    for m in range(64):
        picked = jnp.where(target % 64 == m, order[m], picked)
    choose = iota((256, 256), 1) == picked + target // 64 * 64
    choose = choose.astype(jnp.float32).astype(jnp.bfloat16)
    load.wait()

    @pl.loop(0, 16)
    def _(j):
        at = pl.ds(pl.multiple_of(j * 256, 256), 256)
        sorted_vec = dot(choose, vec[:, at], NT).astype(jnp.bfloat16)
        for a in range(4):
            srt[j * 4 + a] = sorted_vec[a * 64 : a * 64 + 64]

    def orbital(irrep, u):
        return srt[order[irrep * 8 + u]]

    lane = iota((8, 1024), 1)
    for local in range(2):
        pair = core * 2 + local

        @pl.loop(0, 8)
        def _(w):
            for h in range(2):
                at = pl.ds(pl.multiple_of(w * 128 + h * 64, 64), 64)
                brow[at, :] = orbital(xor8(pair * 2 + h, sym), w)

        @pl.loop(0, 8)
        def _(u):
            for h in range(2):
                arow[h * 64 : h * 64 + 64, :] = orbital(pair * 2 + h, u)
            product = dot(arow[...], brow[...], NT)
            wanted = lane // 8 % 16
            total = jnp.zeros((8, 1024), jnp.float32)
            for h in range(2):
                for k in range(8):
                    at = h * 64 + k * 8
                    total = jnp.where(wanted == h * 8 + xor8(k, sym), product[at : at + 8], total)
            for w in range(8):
                gram[w, pl.ds(pl.multiple_of(u * 8, 8), 8), :] = total[:, w * 128 : w * 128 + 128]

        for x in range(8):
            for w in range(8):
                part[local * 64 + w * 8 : local * 64 + w * 8 + 8, x * 128 : x * 128 + 128] = gram[
                    w, pl.ds(x, 8, stride=8), :
                ]

    def rows_of(at):
        return pl.ds(pl.multiple_of(at * 32, 32), 32)

    def along_z(d):
        return pltpu.make_async_remote_copy(
            src_ref=part.at[rows_of((z_at + d) % 4), :],
            dst_ref=gath.at[d - 1],
            send_sem=red_s.at[d],
            recv_sem=red_r.at[d],
            device_id=near(d, 0, 0),
            device_id_type=MESH,
        )

    pl.semaphore_wait(z_sem, 2)
    for d in range(1, 4):
        along_z(d).start()
    total = part[rows_of(z_at), :]
    for d in range(1, 4):
        along_z(d).wait_recv()
        total = total + gath[d - 1]
    mine[...] = total
    along_y = pltpu.make_async_remote_copy(
        src_ref=mine,
        dst_ref=gath.at[3],
        send_sem=red_s.at[0],
        recv_sem=red_r.at[0],
        device_id=near(0, 1, 0),
        device_id_type=MESH,
    )
    along_y.start()
    start_in(FIRST, SECOND)
    along_y.wait_recv()
    place = pl.ds(pl.multiple_of(core * 128 + z_at * 32, 32), 32)
    full[place, :] = (mine[...] + gath[3]).astype(jnp.bfloat16)

    def share(n):
        d, e = others[n]
        return pltpu.make_async_remote_copy(
            src_ref=full.at[place, :],
            dst_ref=full.at[place, :],
            send_sem=all_s.at[n],
            recv_sem=all_r.at[n],
            device_id=near(d, 0, e),
            device_id_type=MESH,
        )

    for n in range(len(others)):
        share(n).start()
    start_in(SECOND, CHUNKS)
    for n in range(len(others)):
        share(n).wait_recv()

    goal, source = iota((1024, 512), 1), iota((1024, 512), 0)
    gk = goal // 64
    other = sum(2**i * ((gk // 2**i % 2 + sym // 2**i % 2) % 2) for i in range(3))
    base = goal // 8 % 8 * 128 + other * 8 + goal % 8
    r, c = iota((256, 256), 0), iota((256, 256), 1)
    swap = c == r // 64 * 64 + r % 8 * 8 + r // 8 % 8
    swap = swap.astype(jnp.float32).astype(jnp.bfloat16)
    for h in range(2):
        pick = (source == base + h * 64).astype(jnp.float32).astype(jnp.bfloat16)
        moved = dot(full[...], pick).astype(jnp.bfloat16)
        moved = dot(swap, moved).astype(jnp.bfloat16)
        for pair in range(4):
            at = (pair * 2 + h) * 64
            ints[at : at + 64, :] = moved[pair * 64 : pair * 64 + 64]

    keep.wait()

    @pl.loop(0, CHUNKS)
    def _(s):
        for i in range(len(PEERS)):
            send_in(i, s).wait_recv()

        @pl.loop(0, step // 256)
        def _(j):
            at = pl.ds(pl.multiple_of(s * step + j * 256, 256), 256)
            out[:, at] = dot(ints[...], slots[:, at]).astype(jnp.bfloat16)

        for i in range(len(PEERS)):
            send_back(i, s).start()
        keep_back(s).start()

    for d in range(1, 4):
        along_z(d).wait_send()
    along_y.wait_send()
    for n in range(len(others)):
        share(n).wait_send()

    @pl.loop(0, CHUNKS)
    def _(s):
        for i in range(len(PEERS)):
            send_in(i, s).wait_send()
        for i in range(len(PEERS)):
            send_back(i, s).wait()
        keep_back(s).wait()


def body(amplitudes, cholesky, virtual_order):
    groups, rows, columns = amplitudes.shape
    width = columns // 2
    sems = pltpu.SemaphoreType.DMA
    peers = len(PEERS)
    vectors = cholesky.shape[0]
    return pl.pallas_call(
        kernel,
        out_shape=pltpu.VMEM(amplitudes.shape, jnp.bfloat16),
        in_specs=[
            pl.BlockSpec(memory_space=pl.ANY),
            pl.BlockSpec(memory_space=pl.ANY),
            pl.BlockSpec(memory_space=pl.ANY),
        ],
        out_specs=pl.BlockSpec(memory_space=pl.ANY),
        scratch_shapes=[
            pltpu.SMEM(virtual_order.shape, jnp.int32),
            pltpu.VMEM((16 * rows, width), jnp.bfloat16),
            pltpu.VMEM((16 * rows, width), jnp.bfloat16),
            pltpu.VMEM(cholesky.shape, jnp.bfloat16),
            pltpu.VMEM((64, 64, vectors), jnp.bfloat16),
            pltpu.VMEM((1024, vectors), jnp.bfloat16),
            pltpu.VMEM((128, vectors), jnp.bfloat16),
            pltpu.VMEM((8, 64, 128), jnp.float32),
            pltpu.VMEM((128, 1024), jnp.float32),
            pltpu.VMEM((4, 32, 1024), jnp.float32),
            pltpu.VMEM((32, 1024), jnp.float32),
            pltpu.VMEM((256, 1024), jnp.bfloat16),
            pltpu.VMEM((512, 512), jnp.bfloat16),
            sems((peers, CHUNKS)),
            sems((peers, CHUNKS)),
            sems((peers, CHUNKS)),
            sems((peers, CHUNKS)),
            sems((4,)),
            sems((4,)),
            sems((7,)),
            sems((7,)),
            sems,
            sems((CHUNKS,)),
            sems,
            sems,
            pltpu.SemaphoreType.REGULAR,
            pltpu.SemaphoreType.REGULAR,
            pltpu.SemaphoreType.REGULAR,
        ],
        compiler_params=pltpu.CompilerParams(
            collective_id=0, has_side_effects=True, vmem_limit_bytes=44000 * 1024
        ),
        name="ladder",
    )(pltpu.with_memory_space_constraint(virtual_order, pltpu.HBM), amplitudes, pltpu.with_memory_space_constraint(cholesky, pltpu.HBM))


def solution(mesh):
    placed = (P(None, "blk", "occ"), P("occ", None), P())
    return jax.shard_map(
        body, mesh=mesh, in_specs=placed, out_specs=P(None, "blk", "occ"), check_vma=False
    )
```

```python
import functools

import jax
import jax.numpy as jnp
from jax import lax
from jax.experimental import pallas as pl
from jax.experimental.pallas import tpu as pltpu
from jax.sharding import PartitionSpec as P

MESH = pl.DeviceIdType.MESH
CHUNKS = 8
EARLY, FIRST, SECOND = 2, 4, 6
HOPS = ((0, 1), (0, 3), (1, 0), (0, 2), (1, 1), (1, 3), (1, 2), (0, 0))
PEERS = tuple((dy, dx, dc) for dc in (0, 1) for dy, dx in HOPS if (dy, dx, dc) != (0, 0, 0))
NEAR = [i for i, at in enumerate(PEERS) if at[:2] in ((0, 1), (0, 3), (1, 0), (0, 0))]
MIDDLE = [i for i, at in enumerate(PEERS) if at[:2] in ((0, 2), (1, 1), (1, 3))]
FAR = [i for i, at in enumerate(PEERS) if at[:2] == (1, 2)]
NT = (((1,), (1,)), ((), ()))


def xor8(a, b):
    return sum(2**i * ((a // 2**i % 2 + b // 2**i % 2) % 2) for i in range(3))


def dot(a, b, dims=(((1,), (0,)), ((), ()))):
    return lax.dot_general(a, b, dims, preferred_element_type=jnp.float32)


def iota(shape, axis):
    return lax.broadcasted_iota(jnp.int32, shape, axis)


def kernel(
    orbitals, amp, chol, res,
    order, slots, out, vec, srt, brow, arow, gram, part, gath, mine, full, ints,
    in_s, in_r, back_s, back_r, red_s, red_r, all_s, all_r, own_in, own_out, vec_sem, order_sem,
    x_sem, z_sem, far_sem,
):
    blk, occ = lax.axis_index("blk"), lax.axis_index("occ")
    y_hi, x_at, core = blk // 8, blk // 2 % 4, blk % 2
    sym, z_at = blk // 2, occ // 2
    width = slots.shape[1]
    step = width // CHUNKS
    rows = slots.shape[0] // 16

    def peer(offset):
        dy, dx, dc = offset
        return (y_hi + dy) % 2 * 8 + (x_at + dx) % 4 * 2 + (core + dc) % 2

    def near(d, f, e):
        return {"blk": sym * 2 + (core + e) % 2, "occ": (z_at + d) % 4 * 2 + (occ + f) % 2}

    others = [(d, e) for e in (0, 1) for d in range(4) if (d, e) != (0, 0)]

    load = pltpu.make_async_copy(chol, vec, vec_sem)
    load.start()
    read = pltpu.make_async_copy(orbitals, order, order_sem)
    read.start()
    keep = pltpu.make_async_copy(
        amp.at[sym, :, pl.ds(pl.multiple_of(core * width, 128), width)],
        slots.at[pl.ds(pl.multiple_of(blk * rows, 32), rows), :],
        own_in,
    )
    keep.start()

    def signal(sem, device):
        pl.semaphore_signal(sem, inc=1, device_id=device, device_id_type=MESH)

    barrier = pltpu.get_barrier_semaphore()
    for i in NEAR:
        signal(barrier, {"blk": peer(PEERS[i])})

    members = [(d, f) for d in range(4) for f in range(2) if (d, f) != (0, 0)]

    @pl.when(occ == 0)
    def _():
        for d, f in members:
            signal(barrier, near(d, f, 0))

    pl.semaphore_wait(barrier, len(NEAR) + jnp.where(occ == 0, 0, 1))

    def columns(half, s):
        return pl.ds(pl.multiple_of(half * width + s * step, 128), step)

    def block(at):
        return pl.ds(pl.multiple_of(at * rows, 32), rows)

    def send_in(i, s):
        to = peer(PEERS[i])
        return pltpu.make_async_remote_copy(
            src_ref=amp.at[to // 2, :, columns(to % 2, s)],
            dst_ref=slots.at[block(blk), columns(0, s)],
            send_sem=in_s.at[i, s],
            recv_sem=in_r.at[i, s],
            device_id={"blk": to},
            device_id_type=MESH,
        )

    def send_back(i, s):
        to = peer(PEERS[i])
        return pltpu.make_async_remote_copy(
            src_ref=out.at[block(to), columns(0, s)],
            dst_ref=res.at[sym, :, columns(core, s)],
            send_sem=back_s.at[i, s],
            recv_sem=back_r.at[i, s],
            device_id={"blk": to},
            device_id_type=MESH,
        )

    def keep_back(s):
        return pltpu.make_async_copy(
            out.at[block(blk), columns(0, s)], res.at[sym, :, columns(core, s)], own_out.at[s]
        )

    def start_in(first, last, which=range(len(PEERS))):
        @pl.loop(first, last)
        def _(s):
            for i in which:
                send_in(i, s).start()

    start_in(0, EARLY, NEAR)
    for dx in (1, 3):
        signal(x_sem, {"blk": peer((0, dx, 0))})

    @pl.when(occ != 0)
    def _():
        signal(z_sem, {"blk": blk, "occ": 0})

    pl.semaphore_wait(x_sem, 2)
    start_in(0, EARLY, MIDDLE)
    signal(far_sem, {"blk": peer((0, 3, 0))})
    pl.semaphore_wait(far_sem, 1)
    start_in(0, EARLY, FAR)
    start_in(EARLY, FIRST)

    read.wait()
    target = iota((256, 1), 0)
    picked = jnp.zeros((256, 1), jnp.int32)
    for m in range(64):
        picked = jnp.where(target % 64 == m, order[m], picked)
    choose = iota((256, 256), 1) == picked + target // 64 * 64
    choose = choose.astype(jnp.float32).astype(jnp.bfloat16)
    load.wait()

    @pl.loop(0, 16)
    def _(j):
        at = pl.ds(pl.multiple_of(j * 256, 256), 256)
        sorted_vec = dot(choose, vec[:, at], NT).astype(jnp.bfloat16)
        for a in range(4):
            srt[j * 4 + a] = sorted_vec[a * 64 : a * 64 + 64]

    def orbital(irrep, u):
        return srt[order[irrep * 8 + u]]

    lane = iota((8, 1024), 1)
    for local in range(2):
        pair = core * 2 + local

        @pl.loop(0, 8)
        def _(w):
            for h in range(2):
                at = pl.ds(pl.multiple_of(w * 128 + h * 64, 64), 64)
                brow[at, :] = orbital(xor8(pair * 2 + h, sym), w)

        @pl.loop(0, 8)
        def _(u):
            for h in range(2):
                arow[h * 64 : h * 64 + 64, :] = orbital(pair * 2 + h, u)
            product = dot(arow[...], brow[...], NT)
            wanted = lane // 8 % 16
            total = jnp.zeros((8, 1024), jnp.float32)
            for h in range(2):
                for k in range(8):
                    at = h * 64 + k * 8
                    total = jnp.where(wanted == h * 8 + xor8(k, sym), product[at : at + 8], total)
            for w in range(8):
                gram[w, pl.ds(pl.multiple_of(u * 8, 8), 8), :] = total[:, w * 128 : w * 128 + 128]

        for x in range(8):
            for w in range(8):
                part[local * 64 + w * 8 : local * 64 + w * 8 + 8, x * 128 : x * 128 + 128] = gram[
                    w, pl.ds(x, 8, stride=8), :
                ]

    def rows_of(at):
        return pl.ds(pl.multiple_of(at * 32, 32), 32)

    def along_z(d):
        return pltpu.make_async_remote_copy(
            src_ref=part.at[rows_of((z_at + d) % 4), :],
            dst_ref=gath.at[d - 1],
            send_sem=red_s.at[d],
            recv_sem=red_r.at[d],
            device_id=near(d, 0, 0),
            device_id_type=MESH,
        )

    @pl.when(occ == 0)
    def _():
        pl.semaphore_wait(z_sem, len(members))
        for d, f in members:
            signal(z_sem, near(d, f, 0))

    @pl.when(occ != 0)
    def _():
        pl.semaphore_wait(z_sem, 1)

    for d in range(1, 4):
        along_z(d).start()
    total = part[rows_of(z_at), :]
    for d in range(1, 4):
        along_z(d).wait_recv()
        total = total + gath[d - 1]
    mine[...] = total
    along_y = pltpu.make_async_remote_copy(
        src_ref=mine,
        dst_ref=gath.at[3],
        send_sem=red_s.at[0],
        recv_sem=red_r.at[0],
        device_id=near(0, 1, 0),
        device_id_type=MESH,
    )
    along_y.start()
    start_in(FIRST, SECOND)
    along_y.wait_recv()
    place = pl.ds(pl.multiple_of(core * 128 + z_at * 32, 32), 32)
    full[place, :] = (mine[...] + gath[3]).astype(jnp.bfloat16)

    def share(n):
        d, e = others[n]
        return pltpu.make_async_remote_copy(
            src_ref=full.at[place, :],
            dst_ref=full.at[place, :],
            send_sem=all_s.at[n],
            recv_sem=all_r.at[n],
            device_id=near(d, 0, e),
            device_id_type=MESH,
        )

    for n in range(len(others)):
        share(n).start()
    start_in(SECOND, CHUNKS)
    for n in range(len(others)):
        share(n).wait_recv()

    goal, source = iota((1024, 512), 1), iota((1024, 512), 0)
    gk = goal // 64
    other = sum(2**i * ((gk // 2**i % 2 + sym // 2**i % 2) % 2) for i in range(3))
    base = goal // 8 % 8 * 128 + other * 8 + goal % 8
    r, c = iota((256, 256), 0), iota((256, 256), 1)
    swap = c == r // 64 * 64 + r % 8 * 8 + r // 8 % 8
    swap = swap.astype(jnp.float32).astype(jnp.bfloat16)
    for h in range(2):
        pick = (source == base + h * 64).astype(jnp.float32).astype(jnp.bfloat16)
        moved = dot(full[...], pick).astype(jnp.bfloat16)
        moved = dot(swap, moved).astype(jnp.bfloat16)
        for pair in range(4):
            at = (pair * 2 + h) * 64
            ints[at : at + 64, :] = moved[pair * 64 : pair * 64 + 64]

    keep.wait()

    @pl.loop(0, CHUNKS)
    def _(s):
        for i in range(len(PEERS)):
            send_in(i, s).wait_recv()

        @pl.loop(0, step // 256)
        def _(j):
            at = pl.ds(pl.multiple_of(s * step + j * 256, 256), 256)
            out[:, at] = dot(ints[...], slots[:, at]).astype(jnp.bfloat16)

        for i in range(len(PEERS)):
            send_back(i, s).start()
        keep_back(s).start()

    for d in range(1, 4):
        along_z(d).wait_send()
    along_y.wait_send()
    for n in range(len(others)):
        share(n).wait_send()

    @pl.loop(0, CHUNKS)
    def _(s):
        for i in range(len(PEERS)):
            send_in(i, s).wait_send()
        for i in range(len(PEERS)):
            send_back(i, s).wait()
        keep_back(s).wait()


def body(amplitudes, cholesky, virtual_order):
    groups, rows, columns = amplitudes.shape
    width = columns // 2
    sems = pltpu.SemaphoreType.DMA
    peers = len(PEERS)
    vectors = cholesky.shape[0]
    return pl.pallas_call(
        kernel,
        out_shape=pltpu.VMEM(amplitudes.shape, jnp.bfloat16),
        in_specs=[
            pl.BlockSpec(memory_space=pl.ANY),
            pl.BlockSpec(memory_space=pl.ANY),
            pl.BlockSpec(memory_space=pl.ANY),
        ],
        out_specs=pl.BlockSpec(memory_space=pl.ANY),
        scratch_shapes=[
            pltpu.SMEM(virtual_order.shape, jnp.int32),
            pltpu.VMEM((16 * rows, width), jnp.bfloat16),
            pltpu.VMEM((16 * rows, width), jnp.bfloat16),
            pltpu.VMEM(cholesky.shape, jnp.bfloat16),
            pltpu.VMEM((64, 64, vectors), jnp.bfloat16),
            pltpu.VMEM((1024, vectors), jnp.bfloat16),
            pltpu.VMEM((128, vectors), jnp.bfloat16),
            pltpu.VMEM((8, 64, 128), jnp.float32),
            pltpu.VMEM((128, 1024), jnp.float32),
            pltpu.VMEM((4, 32, 1024), jnp.float32),
            pltpu.VMEM((32, 1024), jnp.float32),
            pltpu.VMEM((256, 1024), jnp.bfloat16),
            pltpu.VMEM((512, 512), jnp.bfloat16),
            sems((peers, CHUNKS)),
            sems((peers, CHUNKS)),
            sems((peers, CHUNKS)),
            sems((peers, CHUNKS)),
            sems((4,)),
            sems((4,)),
            sems((7,)),
            sems((7,)),
            sems,
            sems((CHUNKS,)),
            sems,
            sems,
            pltpu.SemaphoreType.REGULAR,
            pltpu.SemaphoreType.REGULAR,
            pltpu.SemaphoreType.REGULAR,
        ],
        compiler_params=pltpu.CompilerParams(
            collective_id=0, has_side_effects=True, vmem_limit_bytes=44000 * 1024
        ),
        name="ladder",
    )(pltpu.with_memory_space_constraint(virtual_order, pltpu.HBM), amplitudes, pltpu.with_memory_space_constraint(cholesky, pltpu.HBM))


def solution(mesh):
    placed = (P(None, "blk", "occ"), P("occ", None), P())
    return jax.shard_map(
        body, mesh=mesh, in_specs=placed, out_specs=P(None, "blk", "occ"), check_vma=False
    )
```

```python
import functools

import jax
import jax.numpy as jnp
from jax import lax
from jax.experimental import pallas as pl
from jax.experimental.pallas import tpu as pltpu
from jax.sharding import PartitionSpec as P

MESH = pl.DeviceIdType.MESH
CHUNKS = 8
EARLY, FIRST, SECOND = 2, 4, 6
HOPS = ((0, 1), (0, 3), (1, 0), (0, 2), (1, 1), (1, 3), (1, 2), (0, 0))
PEERS = tuple(
    (dy, dx, (dc + i) % 2)
    for dc in (0, 1)
    for i, (dy, dx) in enumerate(HOPS)
    if (dy, dx, (dc + i) % 2) != (0, 0, 0)
)
NEAR = [i for i, at in enumerate(PEERS) if at[:2] in ((0, 1), (0, 3), (1, 0), (0, 0))]
MIDDLE = [i for i, at in enumerate(PEERS) if at[:2] in ((0, 2), (1, 1), (1, 3))]
FAR = [i for i, at in enumerate(PEERS) if at[:2] == (1, 2)]
NT = (((1,), (1,)), ((), ()))


def xor8(a, b):
    return sum(2**i * ((a // 2**i % 2 + b // 2**i % 2) % 2) for i in range(3))


def dot(a, b, dims=(((1,), (0,)), ((), ()))):
    return lax.dot_general(a, b, dims, preferred_element_type=jnp.float32)


def iota(shape, axis):
    return lax.broadcasted_iota(jnp.int32, shape, axis)


def kernel(
    orbitals, amp, chol, res,
    order, slots, out, vec, srt, brow, arow, gram, part, gath, mine, full, ints,
    in_s, in_r, back_s, back_r, red_s, red_r, all_s, all_r, own_in, own_out, vec_sem, order_sem,
    x_sem, z_sem, far_sem,
):
    blk, occ = lax.axis_index("blk"), lax.axis_index("occ")
    y_hi, x_at, core = blk // 8, blk // 2 % 4, blk % 2
    sym, z_at = blk // 2, occ // 2
    width = slots.shape[1]
    step = width // CHUNKS
    rows = slots.shape[0] // 16

    def peer(offset):
        dy, dx, dc = offset
        return (y_hi + dy) % 2 * 8 + (x_at + dx) % 4 * 2 + (core + dc) % 2

    def near(d, f, e):
        return {"blk": sym * 2 + (core + e) % 2, "occ": (z_at + d) % 4 * 2 + (occ + f) % 2}

    others = [(d, e) for e in (0, 1) for d in range(4) if (d, e) != (0, 0)]

    load = pltpu.make_async_copy(chol, vec, vec_sem)
    load.start()
    read = pltpu.make_async_copy(orbitals, order, order_sem)
    read.start()
    keep = pltpu.make_async_copy(
        amp.at[sym, :, pl.ds(pl.multiple_of(core * width, 128), width)],
        slots.at[pl.ds(pl.multiple_of(blk * rows, 32), rows), :],
        own_in,
    )
    keep.start()

    def signal(sem, device):
        pl.semaphore_signal(sem, inc=1, device_id=device, device_id_type=MESH)

    barrier = pltpu.get_barrier_semaphore()
    for i in NEAR:
        signal(barrier, {"blk": peer(PEERS[i])})

    members = [(d, f) for d in range(4) for f in range(2) if (d, f) != (0, 0)]

    @pl.when(occ == 0)
    def _():
        for d, f in members:
            signal(barrier, near(d, f, 0))

    pl.semaphore_wait(barrier, len(NEAR) + jnp.where(occ == 0, 0, 1))

    def columns(half, s):
        return pl.ds(pl.multiple_of(half * width + s * step, 128), step)

    def block(at):
        return pl.ds(pl.multiple_of(at * rows, 32), rows)

    def send_in(i, s):
        to = peer(PEERS[i])
        return pltpu.make_async_remote_copy(
            src_ref=amp.at[to // 2, :, columns(to % 2, s)],
            dst_ref=slots.at[block(blk), columns(0, s)],
            send_sem=in_s.at[i, s],
            recv_sem=in_r.at[i, s],
            device_id={"blk": to},
            device_id_type=MESH,
        )

    def send_back(i, s):
        to = peer(PEERS[i])
        return pltpu.make_async_remote_copy(
            src_ref=out.at[block(to), columns(0, s)],
            dst_ref=res.at[sym, :, columns(core, s)],
            send_sem=back_s.at[i, s],
            recv_sem=back_r.at[i, s],
            device_id={"blk": to},
            device_id_type=MESH,
        )

    def keep_back(s):
        return pltpu.make_async_copy(
            out.at[block(blk), columns(0, s)], res.at[sym, :, columns(core, s)], own_out.at[s]
        )

    def start_in(first, last, which=range(len(PEERS))):
        @pl.loop(first, last)
        def _(s):
            for i in which:
                send_in(i, s).start()

    start_in(0, EARLY, NEAR)
    for dx in (1, 3):
        signal(x_sem, {"blk": peer((0, dx, 0))})

    @pl.when(occ != 0)
    def _():
        signal(z_sem, {"blk": blk, "occ": 0})

    pl.semaphore_wait(x_sem, 2)
    start_in(0, EARLY, MIDDLE)
    signal(far_sem, {"blk": peer((0, 3, 0))})
    pl.semaphore_wait(far_sem, 1)
    start_in(0, EARLY, FAR)
    start_in(EARLY, FIRST)

    read.wait()
    target = iota((256, 1), 0)
    picked = jnp.zeros((256, 1), jnp.int32)
    for m in range(64):
        picked = jnp.where(target % 64 == m, order[m], picked)
    choose = iota((256, 256), 1) == picked + target // 64 * 64
    choose = choose.astype(jnp.float32).astype(jnp.bfloat16)
    load.wait()

    @pl.loop(0, 16)
    def _(j):
        at = pl.ds(pl.multiple_of(j * 256, 256), 256)
        sorted_vec = dot(choose, vec[:, at], NT).astype(jnp.bfloat16)
        for a in range(4):
            srt[j * 4 + a] = sorted_vec[a * 64 : a * 64 + 64]

    def orbital(irrep, u):
        return srt[order[irrep * 8 + u]]

    lane = iota((8, 1024), 1)
    for local in range(2):
        pair = core * 2 + local

        @pl.loop(0, 8)
        def _(w):
            for h in range(2):
                at = pl.ds(pl.multiple_of(w * 128 + h * 64, 64), 64)
                brow[at, :] = orbital(xor8(pair * 2 + h, sym), w)

        @pl.loop(0, 8)
        def _(u):
            for h in range(2):
                arow[h * 64 : h * 64 + 64, :] = orbital(pair * 2 + h, u)
            product = dot(arow[...], brow[...], NT)
            wanted = lane // 8 % 16
            total = jnp.zeros((8, 1024), jnp.float32)
            for h in range(2):
                for k in range(8):
                    at = h * 64 + k * 8
                    total = jnp.where(wanted == h * 8 + xor8(k, sym), product[at : at + 8], total)
            for w in range(8):
                gram[w, pl.ds(pl.multiple_of(u * 8, 8), 8), :] = total[:, w * 128 : w * 128 + 128]

        for x in range(8):
            for w in range(8):
                part[local * 64 + w * 8 : local * 64 + w * 8 + 8, x * 128 : x * 128 + 128] = gram[
                    w, pl.ds(x, 8, stride=8), :
                ]

    def rows_of(at):
        return pl.ds(pl.multiple_of(at * 32, 32), 32)

    def along_z(d):
        return pltpu.make_async_remote_copy(
            src_ref=part.at[rows_of((z_at + d) % 4), :],
            dst_ref=gath.at[d - 1],
            send_sem=red_s.at[d],
            recv_sem=red_r.at[d],
            device_id=near(d, 0, 0),
            device_id_type=MESH,
        )

    @pl.when(occ == 0)
    def _():
        pl.semaphore_wait(z_sem, len(members))
        for d, f in members:
            signal(z_sem, near(d, f, 0))

    @pl.when(occ != 0)
    def _():
        pl.semaphore_wait(z_sem, 1)

    for d in range(1, 4):
        along_z(d).start()
    total = part[rows_of(z_at), :]
    for d in range(1, 4):
        along_z(d).wait_recv()
        total = total + gath[d - 1]
    mine[...] = total
    along_y = pltpu.make_async_remote_copy(
        src_ref=mine,
        dst_ref=gath.at[3],
        send_sem=red_s.at[0],
        recv_sem=red_r.at[0],
        device_id=near(0, 1, 0),
        device_id_type=MESH,
    )
    along_y.start()
    start_in(FIRST, SECOND)
    along_y.wait_recv()
    place = pl.ds(pl.multiple_of(core * 128 + z_at * 32, 32), 32)
    full[place, :] = (mine[...] + gath[3]).astype(jnp.bfloat16)

    def share(n):
        d, e = others[n]
        return pltpu.make_async_remote_copy(
            src_ref=full.at[place, :],
            dst_ref=full.at[place, :],
            send_sem=all_s.at[n],
            recv_sem=all_r.at[n],
            device_id=near(d, 0, e),
            device_id_type=MESH,
        )

    for n in range(len(others)):
        share(n).start()
    start_in(SECOND, CHUNKS)
    for n in range(len(others)):
        share(n).wait_recv()

    goal, source = iota((1024, 512), 1), iota((1024, 512), 0)
    gk = goal // 64
    other = sum(2**i * ((gk // 2**i % 2 + sym // 2**i % 2) % 2) for i in range(3))
    base = goal // 8 % 8 * 128 + other * 8 + goal % 8
    r, c = iota((256, 256), 0), iota((256, 256), 1)
    swap = c == r // 64 * 64 + r % 8 * 8 + r // 8 % 8
    swap = swap.astype(jnp.float32).astype(jnp.bfloat16)
    for h in range(2):
        pick = (source == base + h * 64).astype(jnp.float32).astype(jnp.bfloat16)
        moved = dot(full[...], pick).astype(jnp.bfloat16)
        moved = dot(swap, moved).astype(jnp.bfloat16)
        for pair in range(4):
            at = (pair * 2 + h) * 64
            ints[at : at + 64, :] = moved[pair * 64 : pair * 64 + 64]

    keep.wait()

    @pl.loop(0, CHUNKS)
    def _(s):
        for i in range(len(PEERS)):
            send_in(i, s).wait_recv()

        @pl.loop(0, step // 256)
        def _(j):
            at = pl.ds(pl.multiple_of(s * step + j * 256, 256), 256)
            out[:, at] = dot(ints[...], slots[:, at]).astype(jnp.bfloat16)

        for i in range(len(PEERS)):
            send_back(i, s).start()
        keep_back(s).start()

    for d in range(1, 4):
        along_z(d).wait_send()
    along_y.wait_send()
    for n in range(len(others)):
        share(n).wait_send()

    @pl.loop(0, CHUNKS)
    def _(s):
        for i in range(len(PEERS)):
            send_in(i, s).wait_send()
        for i in range(len(PEERS)):
            send_back(i, s).wait()
        keep_back(s).wait()


def store(held, res, sem):
    copies = [pltpu.make_async_copy(held.at[g], res.at[g], sem.at[g]) for g in range(held.shape[0])]
    for copy in copies:
        copy.start()
    for copy in copies:
        copy.wait()


def body(amplitudes, cholesky, virtual_order):
    groups, rows, columns = amplitudes.shape
    width = columns // 2
    sems = pltpu.SemaphoreType.DMA
    peers = len(PEERS)
    vectors = cholesky.shape[0]
    result = pl.pallas_call(
        kernel,
        out_shape=pltpu.VMEM(amplitudes.shape, jnp.bfloat16),
        in_specs=[
            pl.BlockSpec(memory_space=pl.ANY),
            pl.BlockSpec(memory_space=pl.ANY),
            pl.BlockSpec(memory_space=pl.ANY),
        ],
        out_specs=pl.BlockSpec(memory_space=pl.ANY),
        scratch_shapes=[
            pltpu.SMEM(virtual_order.shape, jnp.int32),
            pltpu.VMEM((16 * rows, width), jnp.bfloat16),
            pltpu.VMEM((16 * rows, width), jnp.bfloat16),
            pltpu.VMEM(cholesky.shape, jnp.bfloat16),
            pltpu.VMEM((64, 64, vectors), jnp.bfloat16),
            pltpu.VMEM((1024, vectors), jnp.bfloat16),
            pltpu.VMEM((128, vectors), jnp.bfloat16),
            pltpu.VMEM((8, 64, 128), jnp.float32),
            pltpu.VMEM((128, 1024), jnp.float32),
            pltpu.VMEM((4, 32, 1024), jnp.float32),
            pltpu.VMEM((32, 1024), jnp.float32),
            pltpu.VMEM((256, 1024), jnp.bfloat16),
            pltpu.VMEM((512, 512), jnp.bfloat16),
            sems((peers, CHUNKS)),
            sems((peers, CHUNKS)),
            sems((peers, CHUNKS)),
            sems((peers, CHUNKS)),
            sems((4,)),
            sems((4,)),
            sems((7,)),
            sems((7,)),
            sems,
            sems((CHUNKS,)),
            sems,
            sems,
            pltpu.SemaphoreType.REGULAR,
            pltpu.SemaphoreType.REGULAR,
            pltpu.SemaphoreType.REGULAR,
        ],
        compiler_params=pltpu.CompilerParams(
            collective_id=0, has_side_effects=True, vmem_limit_bytes=44000 * 1024
        ),
        name="ladder",
    )(pltpu.with_memory_space_constraint(virtual_order, pltpu.HBM), amplitudes, pltpu.with_memory_space_constraint(cholesky, pltpu.HBM))
    return pl.pallas_call(
        store,
        out_shape=jax.ShapeDtypeStruct(amplitudes.shape, jnp.bfloat16),
        in_specs=[pl.BlockSpec(memory_space=pl.ANY)],
        out_specs=pl.BlockSpec(memory_space=pl.ANY),
        scratch_shapes=[sems((groups,))],
        compiler_params=pltpu.CompilerParams(vmem_limit_bytes=1024 * 1024),
        name="store",
    )(result)


def solution(mesh):
    placed = (P(None, "blk", "occ"), P("occ", None), P())
    return jax.shard_map(
        body, mesh=mesh, in_specs=placed, out_specs=P(None, "blk", "occ"), check_vma=False
    )
```
